32 devices in a mesh: shard: 4 (over y, x), context: 8 (over z, core).
Axes of the slice: x: 2, y: 2, z: 4, core: 2. Of those that a mesh axis runs over, the one named last changes fastest.
Arguments:
- tokens: bfloat16 [4096, 1536], P(('shard', 'context')), may hold values from -6 to 6
- segments: int32 [4096], P(('shard', 'context')), may hold values from 0 to 3, as said below
- positions: int32 [4096], P(('shard', 'context')), may hold values from 0 to 1022, as said below
- attn_gain: float32 [1536], replicated, may hold values from 0.5 to 1.5
- w_qkv: bfloat16 [1536, 2048], P('shard'), may hold values from -0.15625 to 0.15625
- b_qkv: float32 [2048], replicated, may hold values from -3 to 3
- w_out: bfloat16 [1536, 1536], P('shard'), may hold values from -0.625 to 0.625
- ffn_gain: float32 [1536], replicated, may hold values from 0.5 to 1.5
- w_gate_up: bfloat16 [1536, 2, 8960], P('shard', None, 'context'), may hold values from -0.15625 to 0.15625
- w_down: bfloat16 [8960, 1536], P('context', 'shard'), may hold values from -0.1875 to 0.1875
- cotangent: bfloat16 [4096, 1536], P(('shard', 'context')), may hold values from -6 to 6
Outputs:
- output: float32 [4096, 1536], P(('shard', 'context'))
- grad_tokens: float32 [4096, 1536], P(('shard', 'context'))
- grad_attn_gain: float32 [1536], P(('shard', 'context'))
- grad_w_qkv: float32 [1536, 2048], P(('shard', 'context'))
- grad_b_qkv: float32 [2048], P(('shard', 'context'))
- grad_w_out: float32 [1536, 1536], P(('shard', 'context'))
- grad_ffn_gain: float32 [1536], P(('shard', 'context'))
- grad_w_gate_up: float32 [1536, 2, 8960], P('shard', None, 'context')
- grad_w_down: float32 [8960, 1536], P('context', 'shard')
The draws below stay inside these ranges and needn't reach their ends.
Inputs may be any that keep to these rules, and one draw needn't show every extreme that they name: `segments`: segment numbers start at 0 in every sequence, never fall along it (a number may be skipped), and the last token of every sequence has 3. `positions`: a token's position is its index minus the index of the first token of its segment.
All inputs are finite; a program needn't handle non-finite values.
Results may differ from the reference program's by a relative error of at most 0.015.
Values may be sent and summed in bfloat16 or wider, within the bound.
No kernel may reach another device: no remote copies, remote signals or barrier semaphores. Data moves between devices by JAX's collectives and lax.ppermute only.
A program may use at most 192 MiB of HBM per device.

```python
import jax
import jax.numpy as jnp
from jax import lax

D = 1536
HEADS_Q = 12
HEADS_KV = 2
HEAD_DIM = 128
FF = 8960
SEQ = 1024
SEQS = 4
TOKENS = 4096
QKV_W = 2048


def document_cuts(key):
    cuts = jnp.sort(jax.random.randint(jax.random.fold_in(key, 7), (SEQS, 3), 1, SEQ), axis=1)
    first = jnp.arange(SEQS, dtype=jnp.int32)[:, None] == 0
    return jnp.where(first, SEQ - 1, cuts).astype(jnp.int32)


def draw_segments(key, part):
    cuts = document_cuts(key)
    index = jnp.arange(SEQ, dtype=jnp.int32)
    passed = index[None, :, None] >= cuts[:, None, :]
    return jnp.sum(passed.astype(jnp.int32), axis=2).reshape(SEQS * SEQ)


def draw_positions(key, part):
    cuts = document_cuts(key)
    index = jnp.arange(SEQ, dtype=jnp.int32)
    passed = index[None, :, None] >= cuts[:, None, :]
    start = jnp.max(jnp.where(passed, cuts[:, None, :], 0), axis=2)
    return (index[None, :] - start).reshape(SEQS * SEQ)


def draw_b_qkv(key, part):
    return jnp.clip(jax.random.normal(key, (QKV_W,), jnp.float32), -3.0, 3.0)


def with_spikes(array, key, source, target, blocks, factor):
    def block_of(axis_at):
        return (jnp.arange(array.shape[axis_at]) // (array.shape[axis_at] // blocks)).reshape((-1,) + (1,) * (array.ndim - 1 - axis_at))

    near = jax.random.permutation(key, blocks)[block_of(target)]
    far = (block_of(target) + blocks // 2) % blocks
    return jnp.where((block_of(source) == near) | (block_of(source) == far), factor * array, array)


def level_of(own_key, shape, split, least, top_value):
    def one(axis_at, shards_of):
        steps = jax.random.uniform(jax.random.fold_in(jax.random.fold_in(own_key, 6), axis_at), (shards_of,), jnp.float32, least / len(split), top_value / len(split))
        return jnp.repeat(jnp.exp(steps), shape[axis_at] // shards_of).reshape((-1,) + (1,) * (len(shape) - axis_at - 1))

    factor_of = one(*split[0])
    for cut in split[1:]:
        factor_of = factor_of * one(*cut)
    return factor_of


def noise(key, shape, spread, bound, split=(), kind=jnp.bfloat16):
    array = jax.random.normal(key, shape, jnp.float32) * spread
    if len(split) > 0:
        array = level_of(key, shape, split, -0.22, 0.18) * array
    return jnp.clip(array, min=-bound, max=bound).astype(kind)


def noise_with(key, extent, deviation, bound, split, heavy, held_as=jnp.bfloat16):
    entries = deviation * jax.random.normal(key, extent, jnp.float32)
    if split:
        entries = entries * level_of(key, extent, split, -0.22, 0.18)
    return jnp.clip(with_spikes(entries, jax.random.fold_in(key, 3), *heavy), -bound, bound).astype(held_as)


def setup_inputs(seed: int = 0) -> dict:
    splits = jax.random.split(jax.random.key(seed), 12)
    tokens = noise(splits[0], (TOKENS, D), 1.0, 6.0, ((0, 32),))
    segments = draw_segments(jax.random.fold_in(splits[11], 71), 0)
    positions = draw_positions(jax.random.fold_in(splits[11], 71), 0)
    attn_gain = jnp.clip(1.0 + 0.1 * jax.random.normal(splits[3], (D,), jnp.float32), 0.5, 1.5)
    w_qkv = noise(splits[4], (D, QKV_W), D ** -0.5, 0.15625, ((0, 4),))
    b_qkv = draw_b_qkv(jax.random.fold_in(splits[11], 71), 0)
    w_out = noise(splits[6], (D, D), (D // 16) ** -0.5, 0.625, ((0, 4),))
    ffn_gain = jnp.clip(1.0 + 0.1 * jax.random.normal(splits[7], (D,), jnp.float32), 0.5, 1.5)
    w_gate_up = noise(splits[8], (D, 2, FF), D ** -0.5, 0.15625, ((0, 4), (2, 8)))
    w_down = noise_with(splits[9], (FF, D), (FF // 4) ** -0.5, 0.1875, ((0, 8), (1, 4)), (0, 1, 8, 2.0))
    cotangent = noise(splits[10], (TOKENS, D), 1.0, 6.0, ((0, 32),))
    return {"tokens": tokens, "segments": segments, "positions": positions, "attn_gain": attn_gain, "w_qkv": w_qkv, "b_qkv": b_qkv, "w_out": w_out, "ffn_gain": ffn_gain, "w_gate_up": w_gate_up, "w_down": w_down, "cotangent": cotangent}


EPS = 1e-06
THETA = 1000000.0
NEG = -1e+30

def rounded(values):
    return lax.optimization_barrier(values.astype(jnp.bfloat16)).astype(jnp.float32)

def rope_tables(positions):
    half = HEAD_DIM // 2
    frequency = THETA ** (-(jnp.arange(half, dtype=jnp.float32) * (2.0 / HEAD_DIM)))
    angle = positions.astype(jnp.float32)[:, None] * frequency[None, :]
    cosine = jnp.cos(angle)
    sine_part = jnp.sin(angle)
    return (jnp.concatenate([cosine, cosine], 1), jnp.concatenate([sine_part, sine_part], 1))

def rotate(values, cosine, sine_part):
    half = values.shape[-1] // 2
    turned = jnp.concatenate([-values[..., half:], values[..., :half]], -1)
    return values * cosine[:, None, :] + turned * sine_part[:, None, :]

def unrotate(grads, cosine, sine_part):
    half = grads.shape[-1] // 2
    scaled = grads * sine_part[:, None, :]
    return grads * cosine[:, None, :] + jnp.concatenate([scaled[..., half:], -scaled[..., :half]], -1)

def norm_back(values, inverse, weighted):
    return inverse * weighted - values * inverse ** 3 * lax.optimization_barrier(jnp.mean(weighted * values, axis=-1, keepdims=True))

def reference(tokens, segments, positions, attn_gain, w_qkv, b_qkv, w_out, ffn_gain, w_gate_up, w_down, cotangent):
    group = HEADS_Q // HEADS_KV
    q_width = HEADS_Q * HEAD_DIM
    kv_width = HEADS_KV * HEAD_DIM
    block = min(512, SEQ)
    blocks = SEQ // block
    scale = HEAD_DIM ** (-0.5)
    gate_up_flat = w_gate_up.reshape(D, 2 * FF)

    def one_sequence(carry, items):
        seq_tokens, seq_segments, seq_positions, seq_cot = items
        tokens_wide = seq_tokens.astype(jnp.float32)
        inverse_one = lax.rsqrt(lax.optimization_barrier(jnp.mean(tokens_wide * tokens_wide, axis=-1, keepdims=True)) + EPS)
        normed_one = (tokens_wide * inverse_one * attn_gain).astype(jnp.bfloat16)
        projected = jnp.dot(normed_one, w_qkv, preferred_element_type=jnp.float32) + b_qkv
        cosine, sine_part = rope_tables(seq_positions)
        query = rounded(rotate(projected[:, :q_width].reshape(SEQ, HEADS_Q, HEAD_DIM), cosine, sine_part))
        keys = rounded(rotate(projected[:, q_width:q_width + kv_width].reshape(SEQ, HEADS_KV, HEAD_DIM), cosine, sine_part))
        values = rounded(projected[:, q_width + kv_width:].reshape(SEQ, HEADS_KV, HEAD_DIM))
        index = jnp.arange(SEQ, dtype=jnp.int32)
        grouped = query.reshape(SEQ, HEADS_KV, group, HEAD_DIM)

        def scores_for(query_block, query_index, query_seg):
            scores = jnp.einsum('bhgd,jhd->hgbj', query_block, keys) * scale
            allowed = (index[None, :] <= query_index[:, None]) & (seq_segments[None, :] == query_seg[:, None])
            return (jnp.where(allowed[None, None], scores, NEG), allowed)

        def forward_block(args):
            query_block, query_index, query_seg = args
            scores, allowed = scores_for(query_block, query_index, query_seg)
            best = lax.optimization_barrier(jnp.max(scores, axis=-1))
            total = lax.optimization_barrier(jnp.sum(jnp.where(allowed[None, None], jnp.exp(scores - best[..., None]), 0.0), axis=-1))
            lse = best + jnp.log(total)
            probs = rounded(jnp.where(allowed[None, None], jnp.exp(scores - lse[..., None]), 0.0))
            attended = jnp.einsum('hgbj,jhd->bhgd', probs, values)
            return (attended.reshape(block, q_width).astype(jnp.bfloat16), lse)
        query_blocks = grouped.reshape(blocks, block, HEADS_KV, group, HEAD_DIM)
        index_blocks = index.reshape(blocks, block)
        seg_blocks = seq_segments.reshape(blocks, block)
        attended, lse = lax.map(forward_block, (query_blocks, index_blocks, seg_blocks))
        attended = attended.reshape(SEQ, q_width)
        mixed = tokens_wide + jnp.dot(attended, w_out, preferred_element_type=jnp.float32)
        inverse_two = lax.rsqrt(lax.optimization_barrier(jnp.mean(mixed * mixed, axis=-1, keepdims=True)) + EPS)
        normed_two = (mixed * inverse_two * ffn_gain).astype(jnp.bfloat16)
        gate_up = jnp.dot(normed_two, gate_up_flat, preferred_element_type=jnp.float32)
        gate = gate_up[:, :FF]
        upper = gate_up[:, FF:]
        sigma = jax.nn.sigmoid(gate)
        activated = gate * sigma
        hidden = (activated * upper).astype(jnp.bfloat16)
        output = mixed + jnp.dot(hidden, w_down, preferred_element_type=jnp.float32)
        grad_down = jnp.dot(hidden.T, seq_cot, preferred_element_type=jnp.float32)
        grad_hidden = jnp.dot(seq_cot, w_down.T, preferred_element_type=jnp.float32)
        grad_gate = grad_hidden * upper * sigma * (1.0 + gate * (1.0 - sigma))
        grad_upper = grad_hidden * activated
        grad_both = jnp.concatenate([grad_gate, grad_upper], 1).astype(jnp.bfloat16)
        grad_gate_up = jnp.dot(normed_two.T, grad_both, preferred_element_type=jnp.float32)
        grad_normed_two = jnp.dot(grad_both, gate_up_flat.T, preferred_element_type=jnp.float32)
        grad_gain_two = lax.optimization_barrier(jnp.sum(grad_normed_two * mixed * inverse_two, axis=0))
        grad_mixed = seq_cot.astype(jnp.float32) + norm_back(mixed, inverse_two, grad_normed_two * ffn_gain)
        grad_mixed_low = grad_mixed.astype(jnp.bfloat16)
        grad_out_w = jnp.dot(attended.T, grad_mixed_low, preferred_element_type=jnp.float32)
        grad_attended = rounded(jnp.dot(grad_mixed_low, w_out.T, preferred_element_type=jnp.float32))
        grad_grouped = grad_attended.reshape(SEQ, HEADS_KV, group, HEAD_DIM)
        attended_wide = rounded(attended.astype(jnp.float32)).reshape(SEQ, HEADS_KV, group, HEAD_DIM)
        delta = lax.optimization_barrier(jnp.sum(grad_grouped * attended_wide, axis=-1))
        delta_blocks = delta.reshape(blocks, block, HEADS_KV, group).transpose(0, 2, 3, 1)

        def backward_block(acc, args):
            query_block, query_index, query_seg, grad_block, lse_block, delta_block = args
            scores, allowed = scores_for(query_block, query_index, query_seg)
            probs = jnp.where(allowed[None, None], jnp.exp(scores - lse_block[..., None]), 0.0)
            grad_values = jnp.einsum('hgbj,bhgd->jhd', rounded(probs), grad_block)
            grad_probs = jnp.einsum('bhgd,jhd->hgbj', grad_block, values)
            grad_scores = rounded(probs * (grad_probs - delta_block[..., None]))
            grad_query = jnp.einsum('hgbj,jhd->bhgd', grad_scores, keys) * scale
            grad_keys = jnp.einsum('hgbj,bhgd->jhd', grad_scores, query_block) * scale
            return ((acc[0] + grad_keys, acc[1] + grad_values), grad_query)
        zeros_kv = jnp.zeros((SEQ, HEADS_KV, HEAD_DIM), jnp.float32)
        grad_blocks = grad_grouped.reshape(blocks, block, HEADS_KV, group, HEAD_DIM)
        (grad_keys, grad_values), grad_query = lax.scan(backward_block, (zeros_kv, zeros_kv), (query_blocks, index_blocks, seg_blocks, grad_blocks, lse, delta_blocks))
        grad_q = unrotate(grad_query.reshape(SEQ, HEADS_Q, HEAD_DIM), cosine, sine_part).reshape(SEQ, q_width)
        grad_k = unrotate(grad_keys, cosine, sine_part).reshape(SEQ, kv_width)
        grad_projected = jnp.concatenate([grad_q, grad_k, grad_values.reshape(SEQ, kv_width)], 1)
        grad_bias = lax.optimization_barrier(jnp.sum(grad_projected, axis=0))
        grad_projected_low = grad_projected.astype(jnp.bfloat16)
        grad_qkv_w = jnp.dot(normed_one.T, grad_projected_low, preferred_element_type=jnp.float32)
        grad_normed_one = jnp.dot(grad_projected_low, w_qkv.T, preferred_element_type=jnp.float32)
        grad_gain_one = lax.optimization_barrier(jnp.sum(grad_normed_one * tokens_wide * inverse_one, axis=0))
        grad_input = grad_mixed + norm_back(tokens_wide, inverse_one, grad_normed_one * attn_gain)
        carry = (carry[0] + grad_gain_one, carry[1] + grad_qkv_w, carry[2] + grad_bias, carry[3] + grad_out_w, carry[4] + grad_gain_two, carry[5] + grad_gate_up, carry[6] + grad_down)
        return (carry, (output, grad_input))
    init = (jnp.zeros((D,), jnp.float32), jnp.zeros((D, QKV_W), jnp.float32), jnp.zeros((QKV_W,), jnp.float32), jnp.zeros((D, D), jnp.float32), jnp.zeros((D,), jnp.float32), jnp.zeros((D, 2 * FF), jnp.float32), jnp.zeros((FF, D), jnp.float32))
    items = (tokens.reshape(SEQS, SEQ, D), segments.reshape(SEQS, SEQ), positions.reshape(SEQS, SEQ), cotangent.reshape(SEQS, SEQ, D))
    grads, (output, grad_input) = lax.scan(one_sequence, init, items)
    return (output.reshape(TOKENS, D), grad_input.reshape(TOKENS, D), grads[0], grads[1], grads[2], grads[3], grads[4], grads[5].reshape(D, 2, FF), grads[6])
```

```python
import functools

import jax
import jax.numpy as jnp
from jax import lax
from jax.experimental import pallas as pl
from jax.experimental.pallas import tpu as pltpu
from jax.sharding import PartitionSpec as P

D = 1536
HEADS_Q = 12
HEADS_KV = 2
HEAD_DIM = 128
HALF = HEAD_DIM // 2
GROUP = HEADS_Q // HEADS_KV
Q_HALF = GROUP * HEAD_DIM
COLS = Q_HALF + 2 * HEAD_DIM
EPS = 1e-06
THETA = 1000000.0
NEG = -1e30
SCALE = HEAD_DIM**-0.5
F32 = jnp.float32
BF16 = jnp.bfloat16


def nn(a, b):
    return lax.dot_general(a, b, (((1,), (0,)), ((), ())), preferred_element_type=F32)


def nt(a, b):
    return lax.dot_general(a, b, (((1,), (1,)), ((), ())), preferred_element_type=F32)


def tn(a, b):
    return lax.dot_general(a, b, (((0,), (0,)), ((), ())), preferred_element_type=F32)


def xor_shard(block, bits):
    count = lax.axis_size("shard")
    return lax.ppermute(block, "shard", [(i, i ^ bits) for i in range(count)])


def partner(block):
    count = lax.axis_size("context")
    return lax.ppermute(block, "context", [(i, i ^ 1) for i in range(count)])


def gather_blocks(block):
    count = lax.axis_size("shard")
    blocks = {0: block}
    if count == 4:
        cut = block.shape[0] // 2
        blocks[1] = xor_shard(block, 1)
        blocks[2] = xor_shard(block, 2)
        top = xor_shard(blocks[1][:cut], 2)
        low = xor_shard(blocks[2][cut:], 1)
        blocks[3] = jnp.concatenate([top, low], 0)
    else:
        bit = 1
        while bit < count:
            for j in list(blocks):
                blocks[j | bit] = xor_shard(blocks[j], bit)
            bit *= 2
    return [blocks[j] for j in range(count)]


def pick(items, index):
    while len(items) > 1:
        low = (index & 1) == 1
        items = [jnp.where(low, items[i + 1], items[i]) for i in range(0, len(items), 2)]
        index = index >> 1
    return items[0]


def order_of(count):
    return (1, 3, 2, 0) if count == 4 else tuple(range(count))


def to_relative(values, shard, count):
    width = values.shape[1] // count
    blocks = [values[:, i * width : (i + 1) * width] for i in range(count)]
    return jnp.concatenate([pick(blocks, shard ^ j) for j in order_of(count)], 1)


def to_natural(values, shard, count):
    width = values.shape[1] // count
    order = order_of(count)
    blocks = [values[:, order.index(j) * width : (order.index(j) + 1) * width] for j in range(count)]
    return jnp.concatenate([pick(blocks, shard ^ i) for i in range(count)], 1)


def params(**more):
    return pltpu.CompilerParams(vmem_limit_bytes=60 << 20, **more)


def cost(flops, moved):
    return pl.CostEstimate(flops=int(flops), bytes_accessed=int(moved), transcendentals=0)


def project_kernel(count, normed_ref, bias_ref, cos_ref, sin_ref, *refs):
    weights, (query_ref, kv_ref) = refs[:count], refs[count:]
    order = order_of(count)
    width = D // count
    total = None
    for j in range(count):
        at = order.index(j) * width
        part = nn(normed_ref[:, at : at + width], weights[j][...])
        total = part if total is None else total + part
    total = total + bias_ref[...]
    cosine, sine = cos_ref[...], sin_ref[...]
    for h in range(GROUP + 1):
        u = total[:, h * HEAD_DIM : (h + 1) * HEAD_DIM]
        turned = (u * cosine + pltpu.roll(u, HALF, 1) * sine).astype(BF16)
        if h < GROUP:
            query_ref[:, h * HEAD_DIM : (h + 1) * HEAD_DIM] = turned
        else:
            kv_ref[:, :HEAD_DIM] = turned
    kv_ref[:, HEAD_DIM:] = total[:, Q_HALF + HEAD_DIM :].astype(BF16)


def project(normed, bias, cosine, sine, weights):
    rows = normed.shape[0]
    return pl.pallas_call(
        functools.partial(project_kernel, len(weights)),
        out_shape=(
            jax.ShapeDtypeStruct((rows, Q_HALF), BF16),
            jax.ShapeDtypeStruct((rows, 2 * HEAD_DIM), BF16),
        ),
        compiler_params=params(),
        cost_estimate=cost(2 * rows * D * COLS, 2 * D * COLS + 4 * rows * D),
        name="project",
    )(normed, bias, cosine, sine, *weights)


def mask_of(start, seg_row, seg_col, shape):
    key = lax.broadcasted_iota(jnp.int32, shape, 0)
    query = lax.broadcasted_iota(jnp.int32, shape, 1) + start
    return (key <= query) & (seg_col == seg_row)


def attend_kernel(start_ref, query_ref, kv_ref, row_ref, col_ref, out_ref, lse_ref, bias_ref, vt_ref):
    h = pl.program_id(0)

    @pl.when(h == 0)
    def _():
        allowed = mask_of(start_ref[0], row_ref[...], col_ref[...], bias_ref.shape)
        bias_ref[...] = jnp.where(allowed, 0.0, NEG)
        vt_ref[...] = kv_ref[:, HEAD_DIM:].T

    scores = nt(kv_ref[:, :HEAD_DIM], query_ref[...]) * SCALE + bias_ref[...]
    best = jnp.max(scores, axis=0, keepdims=True)
    weights = jnp.exp(scores - best)
    lse = best + jnp.log(jnp.sum(weights, axis=0, keepdims=True))
    lse_ref[0] = jnp.broadcast_to(lse, lse_ref.shape[1:])
    probs = jnp.exp(scores - lse).astype(BF16)
    out_ref[...] = nn(vt_ref[...], probs).T.astype(BF16)


def attend(start, query, kv, seg_row, seg_col):
    rows, keys = query.shape[0], kv.shape[0]
    return pl.pallas_call(
        attend_kernel,
        grid=(GROUP,),
        in_specs=[
            pl.BlockSpec(memory_space=pltpu.SMEM),
            pl.BlockSpec((rows, HEAD_DIM), lambda h: (0, h)),
            pl.BlockSpec((keys, 2 * HEAD_DIM), lambda h: (0, 0)),
            pl.BlockSpec((1, rows), lambda h: (0, 0)),
            pl.BlockSpec((keys, 1), lambda h: (0, 0)),
        ],
        out_specs=(
            pl.BlockSpec((rows, HEAD_DIM), lambda h: (0, h)),
            pl.BlockSpec((1, 8, rows), lambda h: (h, 0, 0)),
        ),
        out_shape=(
            jax.ShapeDtypeStruct((rows, Q_HALF), BF16),
            jax.ShapeDtypeStruct((GROUP, 8, rows), F32),
        ),
        scratch_shapes=[pltpu.VMEM((keys, rows), F32), pltpu.VMEM((HEAD_DIM, keys), BF16)],
        compiler_params=params(),
        cost_estimate=cost(4 * rows * keys * Q_HALF, 4 * (rows * Q_HALF + keys * HEAD_DIM)),
        name="attend",
    )(start, query, kv, seg_row, seg_col)


def attend_back_kernel(
    start_ref, query_ref, kv_ref, row_ref, col_ref, out_ref, grad_ref, lse_ref, cos_ref, sin_ref,
    dq_ref, dsum_ref, dkv_ref, bias_ref, kt_ref, dk_ref, dv_ref,
):
    h = pl.program_id(0)

    @pl.when(h == 0)
    def _():
        allowed = mask_of(start_ref[0], row_ref[...], col_ref[...], bias_ref.shape)
        bias_ref[...] = jnp.where(allowed, 0.0, NEG)
        kt_ref[...] = kv_ref[:, :HEAD_DIM].T
        dk_ref[...] = jnp.zeros_like(dk_ref)
        dv_ref[...] = jnp.zeros_like(dv_ref)

    query, grad = query_ref[...], grad_ref[...]
    delta = jnp.sum((grad.astype(F32) * out_ref[...].astype(F32)).T, axis=0, keepdims=True)
    scores = nt(kv_ref[:, :HEAD_DIM], query) * SCALE + bias_ref[...]
    probs = jnp.exp(scores - lse_ref[0][:1])
    dv_ref[...] += nn(probs.astype(BF16), grad)
    grad_probs = nt(kv_ref[:, HEAD_DIM:], grad)
    grad_scores = (probs * (grad_probs - delta)).astype(BF16)
    dk_ref[...] += nn(grad_scores, query)
    dqt = nn(kt_ref[...], grad_scores) * SCALE
    dq = dqt.T
    dq = dq * cos_ref[...] - pltpu.roll(dq, HALF, 1) * sin_ref[...]
    dsum_ref[...] = jnp.sum(dq, axis=0, keepdims=True)
    dq_ref[...] = dq.astype(BF16)

    @pl.when(h == pl.num_programs(0) - 1)
    def _():
        dkv_ref[:, :HEAD_DIM] = (dk_ref[...] * SCALE).astype(BF16)
        dkv_ref[:, HEAD_DIM:] = dv_ref[...].astype(BF16)


def attend_back(start, query, kv, seg_row, seg_col, attended, grad, lse, cosine, sine):
    rows, keys = query.shape[0], kv.shape[0]
    head = pl.BlockSpec((rows, HEAD_DIM), lambda h: (0, h))
    table = pl.BlockSpec((rows, HEAD_DIM), lambda h: (0, 0))
    return pl.pallas_call(
        attend_back_kernel,
        grid=(GROUP,),
        in_specs=[
            pl.BlockSpec(memory_space=pltpu.SMEM),
            head,
            pl.BlockSpec((keys, 2 * HEAD_DIM), lambda h: (0, 0)),
            pl.BlockSpec((1, rows), lambda h: (0, 0)),
            pl.BlockSpec((keys, 1), lambda h: (0, 0)),
            head,
            head,
            pl.BlockSpec((1, 8, rows), lambda h: (h, 0, 0)),
            table,
            table,
        ],
        out_specs=(
            head,
            pl.BlockSpec((1, HEAD_DIM), lambda h: (0, h)),
            pl.BlockSpec((keys, 2 * HEAD_DIM), lambda h: (0, 0)),
        ),
        out_shape=(
            jax.ShapeDtypeStruct((rows, Q_HALF), BF16),
            jax.ShapeDtypeStruct((1, Q_HALF), F32),
            jax.ShapeDtypeStruct((keys, 2 * HEAD_DIM), BF16),
        ),
        scratch_shapes=[
            pltpu.VMEM((keys, rows), F32),
            pltpu.VMEM((HEAD_DIM, keys), BF16),
            pltpu.VMEM((keys, HEAD_DIM), F32),
            pltpu.VMEM((keys, HEAD_DIM), F32),
        ],
        compiler_params=params(),
        cost_estimate=cost(10 * rows * keys * Q_HALF, 8 * (rows * Q_HALF + keys * HEAD_DIM)),
        name="attend_back",
    )(start, query, kv, seg_row, seg_col, attended, grad, lse, cosine, sine)


TILE = 256


def hidden_kernel(count, chunk, normed_ref, cot_ref, *refs):
    gate_up, down, (out_ref,) = refs[:count], refs[count : 2 * count], refs[2 * count :]
    order = order_of(count)
    width = D // count

    def step(i, _):
        rows = pl.ds(pl.multiple_of(i * chunk, chunk), chunk)
        gate = upper = grad = None
        for j in range(count):
            at = order.index(j) * width
            left = normed_ref[rows, at : at + width]
            g = nt(left, gate_up[j][0])
            u = nt(left, gate_up[j][1])
            d = nt(cot_ref[rows, at : at + width], down[j][...])
            gate = g if gate is None else gate + g
            upper = u if upper is None else upper + u
            grad = d if grad is None else grad + d
        sigma = jax.nn.sigmoid(gate)
        activated = gate * sigma
        out_ref[0, rows, :] = (grad * upper * sigma * (1.0 + gate * (1.0 - sigma))).astype(BF16)
        out_ref[1, rows, :] = (grad * activated).astype(BF16)
        out_ref[2, rows, :] = (activated * upper).astype(BF16)
        return 0

    lax.fori_loop(0, normed_ref.shape[0] // chunk, step, 0)


def hidden_grads(normed, cot, gate_up, down):
    rows, count = normed.shape[0], len(gate_up)
    width = D // count
    units = down[0].shape[0]
    whole = pl.BlockSpec((rows, D), lambda t: (0, 0), pipeline_mode=pl.Buffered(1))
    return pl.pallas_call(
        functools.partial(hidden_kernel, count, 256),
        grid=(pl.cdiv(units, TILE),),
        in_specs=[whole, whole]
        + [pl.BlockSpec((2, TILE, width), lambda t: (0, t, 0))] * count
        + [pl.BlockSpec((TILE, width), lambda t: (t, 0))] * count,
        out_specs=pl.BlockSpec((3, rows, TILE), lambda t: (0, 0, t)),
        out_shape=jax.ShapeDtypeStruct((3, rows, units), BF16),
        compiler_params=params(),
        cost_estimate=cost(6 * rows * D * units, 4 * rows * D + 6 * units * D + 6 * rows * units),
        name="hidden_grads",
    )(normed, cot, *gate_up, *down)


def back_kernel(count, planes, hidden_ref, *refs):
    weights, (out_ref,) = refs[:count], refs[count:]
    order = order_of(count)
    width = D // count
    for j in range(count):
        total = None
        for k in range(planes):
            weight = weights[j][k] if planes > 1 else weights[j][...]
            part = nn(hidden_ref[k], weight)
            total = part if total is None else total + part
        at = order.index(j) * width
        out_ref[:, at : at + width] = total.astype(BF16)


def through(hidden, first, planes, weights):
    count = len(weights)
    rows, units = hidden.shape[1:]
    width = D // count
    tile = 256
    shape = (planes, units, width) if planes > 1 else (units, width)
    return pl.pallas_call(
        functools.partial(back_kernel, count, planes),
        grid=(rows // tile,),
        in_specs=[pl.BlockSpec((planes, tile, units), lambda t: (first // planes, t, 0))]
        + [pl.BlockSpec(shape, lambda t: (0,) * len(shape), pipeline_mode=pl.Buffered(1))] * count,
        out_specs=pl.BlockSpec((tile, D), lambda t: (t, 0)),
        out_shape=jax.ShapeDtypeStruct((rows, D), BF16),
        compiler_params=params(),
        cost_estimate=cost(2 * planes * rows * units * D, 2 * planes * units * (rows + D) + 2 * rows * D),
        name="through",
    )(hidden, *weights)


def project_back_kernel(count, grad_ref, *refs):
    weights, (out_ref,) = refs[:count], refs[count:]
    order = order_of(count)
    width = D // count
    for j in range(count):
        at = order.index(j) * width
        out_ref[:, at : at + width] = nt(grad_ref[...], weights[j][...])


def project_back(grad, weights):
    rows = grad.shape[0]
    return pl.pallas_call(
        functools.partial(project_back_kernel, len(weights)),
        out_shape=jax.ShapeDtypeStruct((rows, D), F32),
        compiler_params=params(),
        cost_estimate=cost(2 * rows * D * COLS, 2 * D * COLS + 6 * rows * D),
        name="project_back",
    )(grad, *weights)


def scatter_grads(first, second, features):
    count = lax.axis_size("shard")
    width = D // count
    if count == 4:
        send_x = tn(first, features[:, : 2 * width]).astype(BF16)
        send_y = tn(second, features[:, width : 3 * width]).astype(BF16)
        got_x = xor_shard(send_x, 1)
        got_y = xor_shard(send_y, 2)
        first_on = (tn(first, features[:, 2 * width : 3 * width]) + got_x[:, width:]).astype(BF16)
        second_on = (tn(second, features[:, :width]) + got_y[:, :width]).astype(BF16)
        last_y = xor_shard(first_on, 2)
        last_x = xor_shard(second_on, 1)
        own = features[:, 3 * width :]
        first_own = tn(first, own) + got_x[:, :width] + last_y
        second_own = tn(second, own) + got_y[:, width:] + last_x
        return first_own, second_own
    both = jnp.concatenate([first, second], 1)
    blocks = {j: tn(both, features[:, j * width : (j + 1) * width]) for j in range(count)}
    bit = count // 2
    while bit:
        for j in [j for j in blocks if j & bit]:
            blocks[j ^ bit] += xor_shard(blocks.pop(j).astype(BF16), bit)
        bit //= 2
    cut = first.shape[1]
    return blocks[0][:cut], blocks[0][cut:]


def half_columns(array, core):
    take = functools.partial(lax.dynamic_slice_in_dim, array, axis=array.ndim - 1)
    return jnp.concatenate(
        [
            take(core * Q_HALF, Q_HALF),
            take(HEADS_Q * HEAD_DIM + core * HEAD_DIM, HEAD_DIM),
            take((HEADS_Q + HEADS_KV) * HEAD_DIM + core * HEAD_DIM, HEAD_DIM),
        ],
        array.ndim - 1,
    )


def norm_back(values, inverse, weighted):
    return inverse * weighted - values * inverse**3 * jnp.mean(
        weighted * values, axis=-1, keepdims=True
    )


def body(
    tokens, segments, positions, attn_gain, w_qkv, b_qkv, w_out, ffn_gain, w_gate_up, w_down, cotangent
):
    rows = tokens.shape[0]
    shards = lax.axis_size("shard")
    length = lax.axis_size("context")
    shard = lax.axis_index("shard")
    place = lax.axis_index("context")
    core = place % 2
    first_core = core == 0
    along = place // 2
    chip_rows = 2 * rows
    same_core = [list(range(k, length, 2)) for k in range(2)]
    start = jnp.reshape(along * chip_rows, (1,)).astype(jnp.int32)

    def on_chip(own):
        other = partner(own)
        return jnp.concatenate(
            [jnp.where(first_core, own, other), jnp.where(first_core, other, own)], 0
        )

    def mine(array):
        return lax.dynamic_slice_in_dim(array, core * rows, rows, 0)

    def others(array):
        return lax.dynamic_slice_in_dim(array, (1 - core) * rows, rows, 0)

    tokens_chip = on_chip(tokens)
    qkv_blocks = gather_blocks(half_columns(w_qkv, core))
    bias_half = half_columns(b_qkv, core)
    out_cols = gather_blocks(lax.dynamic_slice_in_dim(w_out, core * (D // 2), D // 2, 1))
    gate_up_blocks = gather_blocks(jnp.transpose(w_gate_up, (1, 2, 0)))
    down_blocks = gather_blocks(w_down)
    base = shard ^ (core * (shards // 2))
    out_mine = jnp.concatenate([pick(out_cols, base ^ i) for i in range(shards // 2)], 0)
    out_send = jnp.concatenate([pick(out_cols, base ^ i) for i in range(shards // 2, shards)], 0)
    out_got = partner(out_send)
    out_rows = jnp.concatenate(
        [jnp.where(first_core, out_mine, out_got), jnp.where(first_core, out_got, out_mine)], 1
    )

    meta = lax.all_gather(jnp.stack([segments, positions]), "context", axis=0)
    seg_all = meta[:, 0].reshape(-1)
    own_meta = lax.dynamic_slice_in_dim(meta, 2 * along, 2, 0)
    seg_row = own_meta[:, 0].reshape(1, chip_rows)
    seg_col = seg_all[:, None]
    pos_chip = own_meta[:, 1].reshape(chip_rows)
    cot_all = lax.all_gather(to_relative(cotangent, shard, shards), "context", axis=0, tiled=True)
    frequency = THETA ** (-(jnp.arange(HALF, dtype=F32) * (2.0 / HEAD_DIM)))
    angle = pos_chip.astype(F32)[:, None] * frequency[None, :]
    cosine, sine_part = jnp.cos(angle), jnp.sin(angle)
    cosine = jnp.concatenate([cosine, cosine], 1)
    sine = jnp.concatenate([-sine_part, sine_part], 1)

    chip_wide = tokens_chip.astype(F32)
    inverse_chip = lax.rsqrt(jnp.mean(chip_wide * chip_wide, axis=-1, keepdims=True) + EPS)
    normed_one = (chip_wide * inverse_chip * attn_gain).astype(BF16)
    query, kv = project(
        to_relative(normed_one, shard, shards), bias_half[None], cosine, sine, qkv_blocks
    )
    kv_all = lax.all_gather(kv, "context", axis=0, tiled=True, axis_index_groups=same_core)
    attended, lse = attend(start, query, kv_all, seg_row, seg_col)
    out_other = partner(nn(others(attended), out_rows))
    tokens_wide = tokens.astype(F32)
    mixed = tokens_wide + nn(mine(attended), out_rows) + out_other
    inverse_two = lax.rsqrt(jnp.mean(mixed * mixed, axis=-1, keepdims=True) + EPS)
    normed_two = (mixed * inverse_two * ffn_gain).astype(BF16)

    normed_all = lax.all_gather(to_relative(normed_two, shard, shards), "context", axis=0, tiled=True)
    hidden = hidden_grads(normed_all, cot_all, gate_up_blocks, down_blocks)
    grad_normed = lax.psum_scatter(
        through(hidden, 0, 2, gate_up_blocks), "context", scatter_dimension=0, tiled=True
    )
    down_rows = lax.psum_scatter(
        through(hidden, 2, 1, down_blocks), "context", scatter_dimension=0, tiled=True
    )
    cut = hidden.shape[2] // 256 * 128
    grad_down = scatter_grads(hidden[2][:, :cut], hidden[2][:, cut:], cot_all)
    grad_gate_up = scatter_grads(hidden[0], hidden[1], normed_all)
    output = mixed + to_natural(down_rows, shard, shards).astype(F32)
    grad_normed_two = to_natural(grad_normed, shard, shards).astype(F32)
    gain_two = jnp.sum(grad_normed_two * mixed * inverse_two, axis=0)
    grad_mixed = cotangent.astype(F32) + norm_back(mixed, inverse_two, grad_normed_two * ffn_gain)

    mixed_chip = on_chip(grad_mixed.astype(BF16))
    grad_attended = nt(mixed_chip, out_rows).astype(BF16)
    dq, dq_sum, dkv = attend_back(
        start, query, kv_all, seg_row, seg_col, attended, grad_attended, lse, cosine, sine
    )
    dkv = lax.psum_scatter(
        dkv, "context", scatter_dimension=0, tiled=True, axis_index_groups=same_core
    ).astype(F32)
    dk = dkv[:, :HEAD_DIM]
    dk = dk * cosine - jnp.concatenate([dk[:, HALF:], dk[:, :HALF]], 1) * sine
    dkv = jnp.concatenate([dk, dkv[:, HEAD_DIM:]], 1)
    bias_sum = jnp.concatenate([dq_sum[0], jnp.sum(dkv, axis=0)])
    grad_projected = jnp.concatenate([dq, dkv.astype(BF16)], 1)
    back_one = project_back(grad_projected, qkv_blocks)
    back_other = partner(others(back_one))
    grad_normed_one = to_natural(mine(back_one) + back_other, shard, shards)
    inverse_one = mine(inverse_chip)
    gain_one = jnp.sum(grad_normed_one * tokens_wide * inverse_one, axis=0)
    grad_tokens = grad_mixed + norm_back(tokens_wide, inverse_one, grad_normed_one * attn_gain)

    attended_other = partner(attended)
    attended_full = jnp.concatenate(
        [
            jnp.where(first_core, attended, attended_other),
            jnp.where(first_core, attended_other, attended),
        ],
        1,
    )
    out_term = tn(attended_full, lax.dynamic_slice_in_dim(mixed_chip, core * (D // 2), D // 2, 1))
    qkv_term = tn(normed_one, grad_projected)

    def scatter_rows(term):
        term = lax.psum_scatter(term.astype(BF16), "shard", scatter_dimension=0, tiled=True)
        term = lax.psum_scatter(
            term, "context", scatter_dimension=0, tiled=True, axis_index_groups=same_core
        )
        half = term.shape[0] // 2
        own = lax.dynamic_slice_in_dim(term, core * half, half, 0)
        other = partner(lax.dynamic_slice_in_dim(term, (1 - core) * half, half, 0))
        left = jnp.where(first_core, own, other)
        right = jnp.where(first_core, other, own)
        return left, right

    left, right = scatter_rows(jnp.concatenate([qkv_term, out_term], 1))
    grad_qkv = jnp.concatenate(
        [
            left[:, :Q_HALF],
            right[:, :Q_HALF],
            left[:, Q_HALF : Q_HALF + HEAD_DIM],
            right[:, Q_HALF : Q_HALF + HEAD_DIM],
            left[:, Q_HALF + HEAD_DIM : COLS],
            right[:, Q_HALF + HEAD_DIM : COLS],
        ],
        1,
    ).astype(F32)
    grad_out = jnp.concatenate([left[:, COLS:], right[:, COLS:]], 1).astype(F32)

    zero = jnp.zeros((COLS,), F32)
    left = jnp.where(first_core, bias_sum, zero)
    right = jnp.where(first_core, zero, bias_sum)
    bias_full = jnp.concatenate(
        [
            left[:Q_HALF],
            right[:Q_HALF],
            left[Q_HALF : Q_HALF + HEAD_DIM],
            right[Q_HALF : Q_HALF + HEAD_DIM],
            left[Q_HALF + HEAD_DIM :],
            right[Q_HALF + HEAD_DIM :],
        ]
    )
    world = shards * length
    smalls = [gain_one, bias_full, gain_two]
    packed = jnp.concatenate([x.reshape(world, -1) for x in smalls], 1).reshape(-1)
    packed = lax.psum_scatter(packed, ("shard", "context"), scatter_dimension=0, tiled=True)
    a, b = D // world, D // world + b_qkv.shape[0] // world
    return (
        output,
        grad_tokens,
        packed[:a],
        grad_qkv,
        packed[a:b],
        grad_out,
        packed[b:],
        jnp.transpose(jnp.stack(grad_gate_up), (2, 0, 1)),
        jnp.concatenate(grad_down, 0),
    )


def solution(mesh):
    both = ("shard", "context")
    return jax.shard_map(
        body,
        mesh=mesh,
        in_specs=(
            P(both, None),
            P(both),
            P(both),
            P(),
            P("shard", None),
            P(),
            P("shard", None),
            P(),
            P("shard", None, "context"),
            P("context", "shard"),
            P(both, None),
        ),
        out_specs=(
            P(both, None),
            P(both, None),
            P(both),
            P(both, None),
            P(both),
            P(both, None),
            P(both),
            P("shard", None, "context"),
            P("context", "shard"),
        ),
        check_vma=False,
    )
```
